32 devices in a mesh: dom: 32 (over z, y, x, core).
Axes of the slice: x: 2, y: 2, z: 4, core: 2. Of those that a mesh axis runs over, the one named last changes fastest.
Arguments:
- features: bfloat16 [16384, 512], P('dom'), may hold values from -6 to 6
- weight: bfloat16 [512, 512], replicated, may hold values from -0.25 to 0.25
- grad_out: bfloat16 [16384, 512], P('dom'), may hold values from -6 to 6
- adjacency: bfloat16 [768, 128, 128], P('dom'), may hold values from -0.25 to 0.25
- tile_row: int32 [32, 24], P('dom'), may hold values from 0 to 3
- tile_src: int32 [32, 24], P('dom'), may hold values from 0 to 7
- tile_count: int32 [32], P('dom'), may hold values from 1 to 24, as said below
- send_tile: int32 [32, 4], P('dom'), may hold values from 0 to 3
- stale_feat: bfloat16 [32, 4, 128, 512], P('dom'), may hold values from -6 to 6
- stale_grad: bfloat16 [32, 4, 128, 512], P('dom'), may hold values from -6 to 6
- blend: float32 [512], replicated, may hold values from 0.2 to 0.8
Outputs:
- output: bfloat16 [16384, 512], P('dom')
- grad_features: bfloat16 [16384, 512], P('dom')
- grad_weight: bfloat16 [512, 512], replicated
The draws below stay inside these ranges and needn't reach their ends.
Inputs may be any that keep to these rules, and one draw needn't show every extreme that they name: `tile_count`: counts are skewed; some partition holds all 24 entries.
All inputs are finite; a program needn't handle non-finite values.
Results may differ from the reference program's by a relative error of at most 0.0064.
Values may be sent and summed in bfloat16 or wider, within the bound.
A program may use at most 64 MiB of HBM per device.

```python
import jax
import jax.numpy as jnp
from jax import lax

WIDTH = 512
BLOCK = 128
NODES_DEV = 512
TILE_ENT = 24
ROUNDS = 4
TILES_DEV = 4
NODES = 16384
ENTRIES = 768
N_DOM = 32


def draw_tile_count(key, part):
    first_key, second_key = jax.random.split(jax.random.fold_in(key, 17))
    levels = jax.random.randint(first_key, (N_DOM,), 0, 8)
    counts = jnp.maximum(TILE_ENT // (1 + levels), 1)
    chosen = jax.random.randint(second_key, (), 0, N_DOM)
    return counts.at[chosen].set(TILE_ENT).astype(jnp.int32)


def set_ends(array, own_key, low, top_value):
    shape = array.shape
    index_at = [jax.random.randint(jax.random.fold_in(own_key, axis), (), 0, shape[axis]) for axis in range(len(shape))]
    array = array.at[tuple(index_at)].set(low)
    longest = shape.index(max(shape))
    index_at[longest] = (index_at[longest] + 1) % shape[longest]
    return array.at[tuple(index_at)].set(top_value)


def block_scale(rng, extent, cuts, smallest, largest):
    def one(position, parts):
        heights = jax.random.uniform(jax.random.fold_in(jax.random.fold_in(rng, 6), position), (parts,), jnp.float32, smallest / len(cuts), largest / len(cuts))
        return jnp.repeat(jnp.exp(heights), extent[position] // parts).reshape((-1,) + (1,) * (len(extent) - position - 1))

    gain = one(*cuts[0])
    for cut in cuts[1:]:
        gain = gain * one(*cut)
    return gain


def gaussian(rng, dims, width, bound, pieces=(), kind=jnp.bfloat16):
    result = jax.random.normal(rng, dims, jnp.float32) * width
    if len(pieces) > 0:
        result = block_scale(rng, dims, pieces, -0.22, 0.18) * result
    return jnp.clip(result, min=-bound, max=bound).astype(kind)


def setup_inputs(seed: int = 0) -> dict:
    keys = jax.random.split(jax.random.key(seed), 12)
    features = gaussian(keys[0], (NODES, WIDTH), 1.0, 6.0, ((0, 32),))
    weight = gaussian(keys[1], (WIDTH, WIDTH), WIDTH ** -0.5, 0.25)
    grad_out = gaussian(keys[2], (NODES, WIDTH), 1.0, 6.0, ((0, 32),))
    adjacency = gaussian(keys[3], (ENTRIES, BLOCK, BLOCK), (4 * BLOCK) ** -0.5, 0.25, ((0, 32),))
    tile_row = set_ends(jax.random.randint(keys[4], (N_DOM, TILE_ENT), 0, TILES_DEV), jax.random.fold_in(keys[4], 1), 0, TILES_DEV - 1).astype(jnp.int32)
    tile_src = set_ends(jax.random.randint(keys[5], (N_DOM, TILE_ENT), 0, TILES_DEV + ROUNDS), jax.random.fold_in(keys[5], 1), 0, (TILES_DEV + ROUNDS) - 1).astype(jnp.int32)
    tile_count = draw_tile_count(jax.random.fold_in(keys[11], 71), 0)
    send_tile = set_ends(jax.random.randint(keys[7], (N_DOM, ROUNDS), 0, TILES_DEV), jax.random.fold_in(keys[7], 1), 0, TILES_DEV - 1).astype(jnp.int32)
    stale_feat = gaussian(keys[8], (N_DOM, ROUNDS, BLOCK, WIDTH), 1.0, 6.0, ((0, 32),))
    stale_grad = gaussian(keys[9], (N_DOM, ROUNDS, BLOCK, WIDTH), 1.0, 6.0, ((0, 32),))
    blend = jnp.clip(jax.random.uniform(keys[10], (WIDTH,), jnp.float32, 0.2, 0.8), 0.2, 0.8)
    return dict(features=features, weight=weight, grad_out=grad_out, adjacency=adjacency, tile_row=tile_row, tile_src=tile_src, tile_count=tile_count, send_tile=send_tile, stale_feat=stale_feat, stale_grad=stale_grad, blend=blend)


def forward_one(packed):
    table, adj_part, row_ids, src_ids, live_count = packed
    tiles_dev = NODES_DEV // BLOCK
    valid = (jnp.arange(TILE_ENT) < live_count).astype(jnp.float32)
    blocks = table[src_ids].astype(jnp.float32)
    product = jnp.einsum('ecb,ebh->ech', adj_part.astype(jnp.float32), blocks)
    onehot = (row_ids[:, None] == jnp.arange(tiles_dev)[None, :]).astype(jnp.float32) * valid[:, None]
    return jnp.einsum('et,ech->tch', onehot, product).astype(jnp.bfloat16)


def backward_one(packed):
    dz_part, adj_part, row_ids, src_ids, live_count = packed
    tiles_dev = NODES_DEV // BLOCK
    valid = (jnp.arange(TILE_ENT) < live_count).astype(jnp.float32)
    blocks = dz_part[row_ids].astype(jnp.float32)
    product = jnp.einsum('ecb,ech->ebh', adj_part.astype(jnp.float32), blocks)
    onehot = (src_ids[:, None] == jnp.arange(tiles_dev + ROUNDS)[None, :]).astype(jnp.float32) * valid[:, None]
    totals = jnp.einsum('es,ebh->sbh', onehot, product)
    return totals[:tiles_dev], totals[tiles_dev:].astype(jnp.bfloat16)


def reference(features, weight, grad_out, adjacency, tile_row, tile_src, tile_count, send_tile, stale_feat, stale_grad, blend):
    ndev = N_DOM
    tiles_dev = NODES_DEV // BLOCK
    nbits = ndev.bit_length() - 1
    devices = jnp.arange(ndev, dtype=jnp.int32)
    partners = jnp.stack([jnp.bitwise_xor(devices, jnp.int32(1 << (r * nbits // ROUNDS))) for r in range(ROUNDS)], 1)
    round_ids = jnp.arange(ROUNDS, dtype=jnp.int32)[None, :]
    node_tiles = features.reshape(ndev, tiles_dev, BLOCK, WIDTH)
    outgoing = node_tiles[devices[:, None], send_tile]
    fresh = outgoing[partners, round_ids].astype(jnp.float32)
    mixing = blend.astype(jnp.float32)
    used = ((1.0 - mixing) * stale_feat.astype(jnp.float32) + mixing * fresh).astype(jnp.bfloat16)
    table = jnp.concatenate([node_tiles, used], 1)
    adj_all = adjacency.reshape(ndev, TILE_ENT, BLOCK, BLOCK)
    agg = lax.map(forward_one, (table, adj_all, tile_row, tile_src, tile_count))
    agg_flat = agg.reshape(ndev * NODES_DEV, WIDTH)
    pre = jnp.dot(agg_flat, weight, preferred_element_type=jnp.float32)
    sigma = jax.nn.sigmoid(pre)
    output = (pre * sigma).astype(jnp.bfloat16)
    dpre = (grad_out.astype(jnp.float32) * sigma * (1.0 + pre * (1.0 - sigma))).astype(jnp.bfloat16)
    grad_weight = jnp.dot(agg_flat.T, dpre, preferred_element_type=jnp.float32).astype(jnp.bfloat16)
    dagg = jnp.dot(dpre, weight.T, preferred_element_type=jnp.float32).astype(jnp.bfloat16)
    dz_tiles = dagg.reshape(ndev, tiles_dev, BLOCK, WIDTH)
    local_part, sent = lax.map(backward_one, (dz_tiles, adj_all, tile_row, tile_src, tile_count))
    received = sent[partners, round_ids].astype(jnp.float32)
    corrected = (1.0 - mixing) * stale_grad.astype(jnp.float32) + mixing * received
    onehot_send = (send_tile[:, :, None] == jnp.arange(tiles_dev)[None, None, :]).astype(jnp.float32)
    grad_tiles = local_part + jnp.einsum('nrt,nrbh->ntbh', onehot_send, corrected)
    grad_features = grad_tiles.astype(jnp.bfloat16).reshape(ndev * NODES_DEV, WIDTH)
    return output, grad_features, grad_weight
```

```python
import functools

import jax
import jax.numpy as jnp
from jax import lax
from jax.experimental import pallas as pl
from jax.experimental.pallas import tpu as pltpu
from jax.sharding import PartitionSpec as P

MESH = pl.DeviceIdType.MESH
F32 = jnp.float32
BF16 = jnp.bfloat16


def bit_of(i, b):
    return lax.rem(lax.div(i, 1 << b), 2)


def flip(i, mask):
    out = i
    for b in range(mask.bit_length()):
        if mask >> b & 1:
            out = out + (1 - 2 * bit_of(i, b)) * (1 << b)
    return out


class Sems:
    def __init__(self, send, recv):
        self.send, self.recv, self.next = send, recv, 0

    def take(self):
        self.next += 1
        return self.next - 1


def names_and_shapes(tiles, block, width, entries, rounds, n_extra):
    nodes = tiles * block
    half, quarter, piece = width // 2, width // 8, width // 32
    v = pltpu.VMEM
    return dict(
        feat=v((tiles, block, width), BF16),
        wgt=v((width, width), BF16),
        gout=v((nodes, width), BF16),
        adj=v((entries, block, block), BF16),
        sfeat=v((rounds, block, width), BF16),
        sgrad=v((rounds, block, width), BF16),
        fsend=v((rounds, block, width), BF16),
        frecv=v((rounds, block, width), BF16),
        used=v((rounds, block, width), BF16),
        chain=v((entries + 1, block, block), F32),
        dense=v((nodes, (tiles + rounds) * block), BF16),
        part=v((nodes, width), F32),
        agg=v((nodes, width), BF16),
        outv=v((nodes, width), BF16),
        dpre=v((nodes, width), BF16),
        dagg=v((nodes, width), BF16),
        back=v((nodes, width), F32),
        gsend=v((rounds, block, width), BF16),
        grecv=v((rounds, block, width), BF16),
        gfeat=v((nodes, width), BF16),
        s0send=v((half, width), BF16),
        s0recv=v((half, width), BF16),
        acc=v((half, width), F32),
        s1send=v((half, width), BF16),
        s1recv=v((3, quarter, width), BF16),
        s2send=v((3, piece, width), BF16),
        s2recv=v((3, piece, width), BF16),
        xbuf=v((max(n_extra, 1), 4, piece, width), BF16),
        gw=v((width, width), BF16),
        lsem=pltpu.SemaphoreType.DMA((16,)),
        ssem=pltpu.SemaphoreType.DMA((96,)),
        rsem=pltpu.SemaphoreType.DMA((96,)),
    )


def kernel(names, nbits, *refs):
    (features, weight, grad_out, adjacency, stale_feat, stale_grad, blend,
     tile_row, tile_src, tile_count, send_tile, out_hbm, gf_hbm, gw_hbm) = refs[:14]
    s = dict(zip(names, refs[14:]))
    tiles, block, width = s["feat"].shape
    rounds = s["fsend"].shape[0]
    entries = s["adj"].shape[0]
    nodes = tiles * block
    half, quarter, piece = width // 2, width // 8, width // 32
    me = lax.axis_index("dom")
    sems = Sems(s["ssem"], s["rsem"])
    pending = []

    def remote(src, dst, mask):
        i = sems.take()
        c = pltpu.make_async_remote_copy(
            src_ref=src, dst_ref=dst, send_sem=s["ssem"].at[i], recv_sem=s["rsem"].at[i],
            device_id=(flip(me, mask),), device_id_type=MESH)
        c.start()
        pending.append(c)
        return c

    loads = {}
    for i, (src, name) in enumerate((
            (features, "feat"), (adjacency, "adj"), (stale_feat.at[0], "sfeat"),
            (weight, "wgt"), (grad_out, "gout"), (stale_grad.at[0], "sgrad"))):
        loads[name] = pltpu.make_async_copy(src, s[name], s["lsem"].at[i])
        loads[name].start()

    round_mask = [1 << (r * nbits // rounds) for r in range(rounds)]
    extra = []
    b = 5
    while b < nbits:
        extra.append((b, min(2, nbits - b)))
        b += 2
    peers = {1} | {k << 1 for k in (1, 2, 3)} | {k << 3 for k in (1, 2, 3)} | set(round_mask)
    for lo, nb in extra:
        peers |= {k << lo for k in range(1, 1 << nb)}
    barrier = pltpu.get_barrier_semaphore()
    for m in sorted(peers):
        pl.semaphore_signal(barrier, inc=1, device_id=(flip(me, m),), device_id_type=MESH)

    loads["feat"].wait()
    for r in range(rounds):
        s["fsend"][r] = s["feat"][send_tile[0, r]]
    pl.semaphore_wait(barrier, len(peers))
    fcopies = [remote(s["fsend"].at[r], s["frecv"].at[r], round_mask[r]) for r in range(rounds)]

    live = tile_count[0]
    cells = tiles + rounds
    keys = [jnp.where(e < live, tile_row[0, e] * cells + tile_src[0, e], -1 - e) for e in range(entries)]
    loads["adj"].wait()
    s["chain"][0] = jnp.zeros((block, block), F32)
    for e in range(entries):
        prev = jnp.int32(0)
        for f in range(e):
            prev = jnp.where(keys[f] == keys[e], f + 1, prev)
        s["chain"][e + 1] = s["chain"][prev] + s["adj"][e].astype(F32)
    for t in range(tiles):
        for c in range(cells):
            last = jnp.int32(0)
            for e in range(entries):
                last = jnp.where(keys[e] == t * cells + c, e + 1, last)
            s["dense"][t * block:(t + 1) * block, c * block:(c + 1) * block] = s["chain"][last].astype(BF16)

    mix = blend[...]
    keep = 1.0 - mix
    s["part"][...] = jnp.dot(s["dense"][:, :nodes], s["feat"][...].reshape(nodes, width),
                             preferred_element_type=F32)
    loads["sfeat"].wait()
    for r in range(rounds):
        fcopies[r].wait_recv()
        s["used"][r] = (keep * s["sfeat"][r].astype(F32) + mix * s["frecv"][r].astype(F32)).astype(BF16)
    loads["wgt"].wait()
    loads["gout"].wait()
    for t in range(tiles):
        rows = slice(t * block, (t + 1) * block)
        agg = (s["part"][rows, :] + jnp.dot(
            s["dense"][rows, nodes:], s["used"][...].reshape(rounds * block, width),
            preferred_element_type=F32)).astype(BF16)
        s["agg"][rows, :] = agg
        pre = jnp.dot(agg, s["wgt"][...], preferred_element_type=F32)
        sigma = jax.nn.sigmoid(pre)
        s["outv"][rows, :] = (pre * sigma).astype(BF16)
        s["dpre"][rows, :] = (s["gout"][rows, :].astype(F32) * sigma * (1.0 + pre * (1.0 - sigma))).astype(BF16)
    out_copy = pltpu.make_async_copy(s["outv"], out_hbm, s["lsem"].at[8])
    out_copy.start()

    j0 = bit_of(me, 0)
    j1 = lax.rem(lax.div(me, 2), 4)
    j2 = lax.rem(lax.div(me, 8), 4)

    def half_product(h):
        cols = pl.ds(pl.multiple_of(h * half, half), half)
        return lax.dot_general(s["agg"][:, cols], s["dpre"][...], (((0,), (0,)), ((), ())),
                               preferred_element_type=F32)

    def quarter_rows(k):
        return pl.ds(pl.multiple_of(flip(j1, k) * quarter, quarter), quarter)

    def piece_rows(k, base=0):
        return pl.ds(pl.multiple_of(base + flip(j2, k) * piece, piece), piece)

    s["s0send"][...] = half_product(1 - j0).astype(BF16)
    order1 = (3, 1, 2, 0)
    core = {}
    for k in order1:
        core[k] = remote(s["s0send"].at[quarter_rows(k)], s["s0recv"].at[quarter_rows(k)], 1)
    s["acc"][...] = half_product(j0)
    plane = {}
    for k in order1:
        core[k].wait_recv()
        total = s["acc"][quarter_rows(k), :] + s["s0recv"][quarter_rows(k), :].astype(F32)
        if k == 0:
            s["acc"][quarter_rows(0), :] = total
            continue
        s["s1send"][quarter_rows(k), :] = total.astype(BF16)
        for kz in (3, 2, 1, 0):
            plane[k, kz] = remote(s["s1send"].at[piece_rows(kz, flip(j1, k) * quarter)],
                                  s["s1recv"].at[k - 1, piece_rows(kz)], k << 1)

    s["dagg"][...] = lax.dot_general(s["dpre"][...], s["wgt"][...], (((1,), (1,)), ((), ())),
                                     preferred_element_type=F32).astype(BF16)
    s["gsend"][...] = lax.dot_general(s["dense"][:, nodes:], s["dagg"][...], (((0,), (0,)), ((), ())),
                                      preferred_element_type=F32).astype(BF16).reshape(rounds, block, width)
    gcopies = {}
    late = [r for r in range(rounds) if round_mask[r] in (2, 4)]
    for r in range(rounds):
        if r not in late:
            gcopies[r] = remote(s["gsend"].at[r], s["grecv"].at[r], round_mask[r])
    s["back"][...] = lax.dot_general(s["dense"][:, :nodes], s["dagg"][...], (((0,), (0,)), ((), ())),
                                     preferred_element_type=F32)

    line = {}
    for kz in (3, 2, 1, 0):
        total = s["acc"][piece_rows(kz, j1 * quarter), :]
        for k in (1, 2, 3):
            plane[k, kz].wait_recv()
            total = total + s["s1recv"][k - 1, piece_rows(kz), :].astype(F32)
        if kz:
            s["s2send"][kz - 1] = total.astype(BF16)
            line[kz] = remote(s["s2send"].at[kz - 1], s["s2recv"].at[kz - 1], kz << 3)
    for r in late:
        gcopies[r] = remote(s["gsend"].at[r], s["grecv"].at[r], round_mask[r])
    for kz in (1, 2, 3):
        line[kz].wait_recv()
        total = total + s["s2recv"][kz - 1].astype(F32)
    for g, (lo, nb) in enumerate(extra):
        size = 1 << nb
        jx = lax.rem(lax.div(me, 1 << lo), size)
        s["xbuf"][g, pl.ds(jx, 1)] = total.astype(BF16)[None]
        swaps = [remote(s["xbuf"].at[g, jx], s["xbuf"].at[g, jx], k << lo) for k in range(1, size)]
        for c in swaps:
            c.wait_recv()
        total = s["xbuf"][g, 0].astype(F32)
        for x in range(1, size):
            total = total + s["xbuf"][g, x].astype(F32)

    def gw_rows(kc, kp, kz):
        at = flip(j0, kc) * half + flip(j1, kp) * quarter + flip(j2, kz) * piece
        return pl.ds(pl.multiple_of(at, piece), piece)

    arrivals = {}

    def forward(kc, kp, kz, level):
        ref = s["gw"].at[gw_rows(kc, kp, kz)]
        if level > 2:
            for k in (3, 2, 1):
                arrivals[kc, kp, k] = remote(ref, ref, k << 3)
        if level > 1:
            for k in (3, 1, 2):
                arrivals[kc, k, kz] = remote(ref, ref, k << 1)
        arrivals[1, kp, kz] = remote(ref, ref, 1)

    s["gw"][gw_rows(0, 0, 0), :] = total.astype(BF16)
    forward(0, 0, 0, 3)

    loads["sgrad"].wait()
    hot = [[jnp.where(send_tile[0, r] == t, 1.0, 0.0).astype(F32) for r in range(rounds)] for t in range(tiles)]
    for r in range(rounds):
        gcopies[r].wait_recv()
        corrected = keep * s["sgrad"][r].astype(F32) + mix * s["grecv"][r].astype(F32)
        for t in range(tiles):
            rows = slice(t * block, (t + 1) * block)
            s["back"][rows, :] = s["back"][rows, :] + hot[t][r] * corrected
    s["gfeat"][...] = s["back"][...].astype(BF16)
    gf_copy = pltpu.make_async_copy(s["gfeat"], gf_hbm, s["lsem"].at[9])
    gf_copy.start()

    for kz in (1, 2, 3):
        arrivals[0, 0, kz].wait_recv()
        forward(0, 0, kz, 2)
    for kz in (0, 1, 2, 3):
        for kp in (1, 2, 3):
            arrivals[0, kp, kz].wait_recv()
            forward(0, kp, kz, 1)
    for kz in range(4):
        for kp in range(4):
            arrivals[1, kp, kz].wait_recv()
    gw_copy = pltpu.make_async_copy(s["gw"], gw_hbm, s["lsem"].at[10])
    gw_copy.start()
    for c in pending:
        c.wait_send()
    out_copy.wait()
    gf_copy.wait()
    gw_copy.wait()


def body(nbits, features, weight, grad_out, adjacency, tile_row, tile_src, tile_count,
         send_tile, stale_feat, stale_grad, blend):
    nodes, width = features.shape
    entries, block = adjacency.shape[:2]
    rounds = send_tile.shape[1]
    tiles = nodes // block
    n_extra = (max(nbits - 5, 0) + 1) // 2
    scratch = names_and_shapes(tiles, block, width, entries, rounds, n_extra)
    hbm = pl.BlockSpec(memory_space=pl.ANY)
    smem = pl.BlockSpec(memory_space=pltpu.SMEM)
    vmem = pl.BlockSpec(memory_space=pltpu.VMEM)
    out, gf, gw = pl.pallas_call(
        functools.partial(kernel, tuple(scratch), nbits),
        name="layer",
        out_shape=(jax.ShapeDtypeStruct((nodes, width), BF16),
                   jax.ShapeDtypeStruct((nodes, width), BF16),
                   jax.ShapeDtypeStruct((width, width), BF16)),
        in_specs=[hbm] * 6 + [vmem] + [smem] * 4,
        out_specs=(hbm, hbm, hbm),
        scratch_shapes=list(scratch.values()),
        compiler_params=pltpu.CompilerParams(collective_id=0, has_side_effects=True,
                                             vmem_limit_bytes=48 * 1024 * 1024),
    )(features.reshape(tiles, block, width), weight, grad_out, adjacency, stale_feat, stale_grad,
      blend.reshape(1, width), tile_row, tile_src, tile_count, send_tile)
    return out, gf, gw


def solution(mesh):
    nbits = mesh.shape["dom"].bit_length() - 1
    placed = (
        P("dom", None), P(), P("dom", None), P("dom", None, None), P("dom", None), P("dom", None),
        P("dom"), P("dom", None), P("dom", None, None, None), P("dom", None, None, None), P(),
    )
    return jax.shard_map(
        functools.partial(body, nbits),
        mesh=mesh,
        in_specs=placed,
        out_specs=(P("dom", None), P("dom", None), P()),
        check_vma=False,
    )
```

```python
import functools

import jax
import jax.numpy as jnp
from jax import lax
from jax.experimental import pallas as pl
from jax.experimental.pallas import tpu as pltpu
from jax.sharding import PartitionSpec as P

MESH = pl.DeviceIdType.MESH
F32 = jnp.float32
BF16 = jnp.bfloat16


def bit_of(i, b):
    return lax.rem(lax.div(i, 1 << b), 2)


def flip(i, mask):
    out = i
    for b in range(mask.bit_length()):
        if mask >> b & 1:
            out = out + (1 - 2 * bit_of(i, b)) * (1 << b)
    return out


class Sems:
    def __init__(self, send, recv):
        self.send, self.recv, self.next = send, recv, 0

    def take(self):
        self.next += 1
        return self.next - 1


def names_and_shapes(tiles, block, width, entries, rounds, n_extra):
    nodes = tiles * block
    half, quarter, piece = width // 2, width // 8, width // 32
    v = pltpu.VMEM
    return dict(
        feat=v((tiles, block, width), BF16),
        wgt=v((width, width), BF16),
        gout=v((nodes, width), BF16),
        adj=v((entries, block, block), BF16),
        sfeat=v((rounds, block, width), BF16),
        sgrad=v((rounds, block, width), BF16),
        fsend=v((rounds, block, width), BF16),
        frecv=v((rounds, block, width), BF16),
        used=v((rounds, block, width), BF16),
        chain=v((entries + 1, block, block), F32),
        dense=v((nodes, (tiles + rounds) * block), BF16),
        part=v((nodes, width), F32),
        agg=v((nodes, width), BF16),
        outv=v((nodes, width), BF16),
        dpre=v((nodes, width), BF16),
        dagg=v((nodes, width), BF16),
        back=v((nodes, width), F32),
        gsend=v((rounds, block, width), BF16),
        grecv=v((rounds, block, width), BF16),
        gfeat=v((nodes, width), BF16),
        s0send=v((half, width), BF16),
        s0recv=v((half, width), BF16),
        acc=v((half, width), F32),
        s1send=v((half, width), BF16),
        s1recv=v((3, quarter, width), BF16),
        s2send=v((3, piece, width), BF16),
        s2recv=v((3, piece, width), BF16),
        xbuf=v((max(n_extra, 1), 4, piece, width), BF16),
        mine=v((piece, width), BF16),
        mixv=v((1, width), F32),
        row_s=pltpu.SMEM((1, entries), jnp.int32),
        src_s=pltpu.SMEM((1, entries), jnp.int32),
        tile_s=pltpu.SMEM((1, rounds), jnp.int32),
        lsem=pltpu.SemaphoreType.DMA((16,)),
        ssem=pltpu.SemaphoreType.DMA((96,)),
        rsem=pltpu.SemaphoreType.DMA((96,)),
    )


def kernel(names, nbits, *refs):
    (features, weight, grad_out, adjacency, stale_feat, stale_grad, blend,
     row_hbm, src_hbm, tile_hbm, tile_count, out_any, gf_any, gw_any) = refs[:14]
    s = dict(zip(names, refs[14:]))
    tile_row, tile_src, send_tile = s["row_s"], s["src_s"], s["tile_s"]
    tiles, block, width = s["feat"].shape
    rounds = s["fsend"].shape[0]
    entries = s["adj"].shape[0]
    nodes = tiles * block
    half, quarter, piece = width // 2, width // 8, width // 32
    me = lax.axis_index("dom")
    sems = Sems(s["ssem"], s["rsem"])
    pending = []

    def remote(src, dst, mask):
        i = sems.take()
        c = pltpu.make_async_remote_copy(
            src_ref=src, dst_ref=dst, send_sem=s["ssem"].at[i], recv_sem=s["rsem"].at[i],
            device_id=(flip(me, mask),), device_id_type=MESH)
        c.start()
        pending.append(c)
        return c

    loads = {}
    for i, (src, name) in enumerate((
            (tile_hbm, "tile_s"), (features, "feat"), (row_hbm, "row_s"), (src_hbm, "src_s"),
            (adjacency, "adj"), (blend, "mixv"), (stale_feat.at[0], "sfeat"),
            (weight, "wgt"), (grad_out, "gout"), (stale_grad.at[0], "sgrad"))):
        loads[name] = pltpu.make_async_copy(src, s[name], s["lsem"].at[i])
        loads[name].start()

    round_mask = [1 << (r * nbits // rounds) for r in range(rounds)]
    extra = []
    b = 5
    while b < nbits:
        extra.append((b, min(2, nbits - b)))
        b += 2
    peers = {1} | {k << 1 for k in (1, 2, 3)} | {k << 3 for k in (1, 2, 3)} | set(round_mask)
    for lo, nb in extra:
        peers |= {k << lo for k in range(1, 1 << nb)}
    barrier = pltpu.get_barrier_semaphore()
    for m in sorted(peers):
        pl.semaphore_signal(barrier, inc=1, device_id=(flip(me, m),), device_id_type=MESH)

    loads["tile_s"].wait()
    loads["feat"].wait()
    for r in range(rounds):
        s["fsend"][r] = s["feat"][send_tile[0, r]]
    pl.semaphore_wait(barrier, len(peers))
    fcopies = [remote(s["fsend"].at[r], s["frecv"].at[r], round_mask[r]) for r in range(rounds)]

    for name in ("row_s", "src_s"):
        loads[name].wait()
    live = tile_count[0]
    cells = tiles + rounds
    keys = [jnp.where(e < live, tile_row[0, e] * cells + tile_src[0, e], -1 - e) for e in range(entries)]
    loads["adj"].wait()
    s["chain"][0] = jnp.zeros((block, block), F32)
    for e in range(entries):
        prev = jnp.int32(0)
        for f in range(e):
            prev = jnp.where(keys[f] == keys[e], f + 1, prev)
        s["chain"][e + 1] = s["chain"][prev] + s["adj"][e].astype(F32)
    for t in range(tiles):
        for c in range(cells):
            last = jnp.int32(0)
            for e in range(entries):
                last = jnp.where(keys[e] == t * cells + c, e + 1, last)
            s["dense"][t * block:(t + 1) * block, c * block:(c + 1) * block] = s["chain"][last].astype(BF16)

    loads["mixv"].wait()
    mix = s["mixv"][...]
    keep = 1.0 - mix
    s["part"][...] = jnp.dot(s["dense"][:, :nodes], s["feat"][...].reshape(nodes, width),
                             preferred_element_type=F32)
    loads["sfeat"].wait()
    for r in range(rounds):
        fcopies[r].wait_recv()
        s["used"][r] = (keep * s["sfeat"][r].astype(F32) + mix * s["frecv"][r].astype(F32)).astype(BF16)
    loads["wgt"].wait()
    loads["gout"].wait()
    for t in range(tiles):
        rows = slice(t * block, (t + 1) * block)
        agg = (s["part"][rows, :] + jnp.dot(
            s["dense"][rows, nodes:], s["used"][...].reshape(rounds * block, width),
            preferred_element_type=F32)).astype(BF16)
        s["agg"][rows, :] = agg
        pre = jnp.dot(agg, s["wgt"][...], preferred_element_type=F32)
        sigma = jax.nn.sigmoid(pre)
        s["outv"][rows, :] = (pre * sigma).astype(BF16)
        s["dpre"][rows, :] = (s["gout"][rows, :].astype(F32) * sigma * (1.0 + pre * (1.0 - sigma))).astype(BF16)
    out_copy = pltpu.make_async_copy(s["outv"], out_any, s["lsem"].at[12])
    out_copy.start()

    j0 = bit_of(me, 0)
    j1 = lax.rem(lax.div(me, 2), 4)
    j2 = lax.rem(lax.div(me, 8), 4)

    def half_product(h):
        cols = pl.ds(pl.multiple_of(h * half, half), half)
        return lax.dot_general(s["agg"][:, cols], s["dpre"][...], (((0,), (0,)), ((), ())),
                               preferred_element_type=F32)

    def quarter_rows(k):
        return pl.ds(pl.multiple_of(flip(j1, k) * quarter, quarter), quarter)

    def piece_rows(k, base=0):
        return pl.ds(pl.multiple_of(base + flip(j2, k) * piece, piece), piece)

    s["s0send"][...] = half_product(1 - j0).astype(BF16)
    order1 = (3, 1, 2, 0)
    core = {}
    for k in order1:
        core[k] = remote(s["s0send"].at[quarter_rows(k)], s["s0recv"].at[quarter_rows(k)], 1)
    s["acc"][...] = half_product(j0)
    plane = {}
    for k in order1:
        core[k].wait_recv()
        total = s["acc"][quarter_rows(k), :] + s["s0recv"][quarter_rows(k), :].astype(F32)
        if k == 0:
            s["acc"][quarter_rows(0), :] = total
            continue
        s["s1send"][quarter_rows(k), :] = total.astype(BF16)
        for kz in (3, 2, 1, 0):
            plane[k, kz] = remote(s["s1send"].at[piece_rows(kz, flip(j1, k) * quarter)],
                                  s["s1recv"].at[k - 1, piece_rows(kz)], k << 1)

    s["dagg"][...] = lax.dot_general(s["dpre"][...], s["wgt"][...], (((1,), (1,)), ((), ())),
                                     preferred_element_type=F32).astype(BF16)
    s["gsend"][...] = lax.dot_general(s["dense"][:, nodes:], s["dagg"][...], (((0,), (0,)), ((), ())),
                                      preferred_element_type=F32).astype(BF16).reshape(rounds, block, width)
    gcopies = {}
    late = [r for r in range(rounds) if round_mask[r] in (2, 4)]
    for r in range(rounds):
        if r not in late:
            gcopies[r] = remote(s["gsend"].at[r], s["grecv"].at[r], round_mask[r])
    s["back"][...] = lax.dot_general(s["dense"][:, :nodes], s["dagg"][...], (((0,), (0,)), ((), ())),
                                     preferred_element_type=F32)

    line = {}
    for kz in (3, 2, 1, 0):
        total = s["acc"][piece_rows(kz, j1 * quarter), :]
        for k in (1, 2, 3):
            plane[k, kz].wait_recv()
            total = total + s["s1recv"][k - 1, piece_rows(kz), :].astype(F32)
        if kz:
            s["s2send"][kz - 1] = total.astype(BF16)
            line[kz] = remote(s["s2send"].at[kz - 1], s["s2recv"].at[kz - 1], kz << 3)
    for r in late:
        gcopies[r] = remote(s["gsend"].at[r], s["grecv"].at[r], round_mask[r])
    for kz in (1, 2, 3):
        line[kz].wait_recv()
        total = total + s["s2recv"][kz - 1].astype(F32)
    for g, (lo, nb) in enumerate(extra):
        size = 1 << nb
        jx = lax.rem(lax.div(me, 1 << lo), size)
        s["xbuf"][g, pl.ds(jx, 1)] = total.astype(BF16)[None]
        swaps = [remote(s["xbuf"].at[g, jx], s["xbuf"].at[g, jx], k << lo) for k in range(1, size)]
        for c in swaps:
            c.wait_recv()
        total = s["xbuf"][g, 0].astype(F32)
        for x in range(1, size):
            total = total + s["xbuf"][g, x].astype(F32)

    def gw_rows(kc, kp, kz):
        at = flip(j0, kc) * half + flip(j1, kp) * quarter + flip(j2, kz) * piece
        return pl.ds(pl.multiple_of(at, piece), piece)

    arrivals = {}

    def forward(kc, kp, kz, level):
        dst = gw_any.at[gw_rows(kc, kp, kz)]
        ref = s["mine"] if level > 2 else dst
        if level > 2:
            for k in (3, 2, 1):
                arrivals[kc, kp, k] = remote(ref, dst, k << 3)
        if level > 1:
            for k in (3, 1, 2):
                arrivals[kc, k, kz] = remote(ref, dst, k << 1)
        arrivals[1, kp, kz] = remote(ref, dst, 1)

    s["mine"][...] = total.astype(BF16)
    forward(0, 0, 0, 3)
    own = pltpu.make_async_copy(s["mine"], gw_any.at[gw_rows(0, 0, 0)], s["lsem"].at[14])
    own.start()

    loads["sgrad"].wait()
    hot = [[jnp.where(send_tile[0, r] == t, 1.0, 0.0).astype(F32) for r in range(rounds)] for t in range(tiles)]
    for r in range(rounds):
        gcopies[r].wait_recv()
        corrected = keep * s["sgrad"][r].astype(F32) + mix * s["grecv"][r].astype(F32)
        for t in range(tiles):
            rows = slice(t * block, (t + 1) * block)
            s["back"][rows, :] = s["back"][rows, :] + hot[t][r] * corrected
    s["gfeat"][...] = s["back"][...].astype(BF16)
    gf_copy = pltpu.make_async_copy(s["gfeat"], gf_any, s["lsem"].at[13])
    gf_copy.start()

    for kz in (1, 2, 3):
        arrivals[0, 0, kz].wait_recv()
        forward(0, 0, kz, 2)
    for kz in (0, 1, 2, 3):
        for kp in (1, 2, 3):
            arrivals[0, kp, kz].wait_recv()
            forward(0, kp, kz, 1)
    for kz in range(4):
        for kp in range(4):
            arrivals[1, kp, kz].wait_recv()
    for c in pending:
        c.wait_send()
    own.wait()
    out_copy.wait()
    gf_copy.wait()


def finish(*refs):
    ins, outs, sem = refs[:3], refs[3:6], refs[6]
    copies = [pltpu.make_async_copy(a, b, sem.at[i]) for i, (a, b) in enumerate(zip(ins, outs))]
    for c in copies:
        c.start()
    for c in copies:
        c.wait()


def body(nbits, features, weight, grad_out, adjacency, tile_row, tile_src, tile_count,
         send_tile, stale_feat, stale_grad, blend):
    nodes, width = features.shape
    entries, block = adjacency.shape[:2]
    rounds = send_tile.shape[1]
    tiles = nodes // block
    n_extra = (max(nbits - 5, 0) + 1) // 2
    scratch = names_and_shapes(tiles, block, width, entries, rounds, n_extra)
    hbm = pl.BlockSpec(memory_space=pltpu.HBM)
    free = pl.BlockSpec(memory_space=pl.ANY)
    results = (jax.ShapeDtypeStruct((nodes, width), BF16),
               jax.ShapeDtypeStruct((nodes, width), BF16),
               jax.ShapeDtypeStruct((width, width), BF16))
    found = pl.pallas_call(
        functools.partial(kernel, tuple(scratch), nbits),
        name="layer",
        out_shape=results,
        in_specs=[hbm] * 10 + [pl.BlockSpec(memory_space=pltpu.SMEM)],
        out_specs=(free,) * 3,
        scratch_shapes=list(scratch.values()),
        compiler_params=pltpu.CompilerParams(collective_id=0, has_side_effects=True,
                                             vmem_limit_bytes=48 * 1024 * 1024),
    )(*(pltpu.with_memory_space_constraint(x, pltpu.HBM) for x in (
        features.reshape(tiles, block, width), weight, grad_out, adjacency, stale_feat, stale_grad,
        blend.reshape(1, width), tile_row, tile_src, send_tile)), tile_count)
    return tuple(pl.pallas_call(
        finish,
        name="finish",
        out_shape=results,
        in_specs=[free] * 3,
        out_specs=(hbm,) * 3,
        scratch_shapes=[pltpu.SemaphoreType.DMA((3,))],
        compiler_params=pltpu.CompilerParams(vmem_limit_bytes=16 * 1024 * 1024),
    )(*found))


def solution(mesh):
    nbits = mesh.shape["dom"].bit_length() - 1
    placed = (
        P("dom", None), P(), P("dom", None), P("dom", None, None), P("dom", None), P("dom", None),
        P("dom"), P("dom", None), P("dom", None, None, None), P("dom", None, None, None), P(),
    )
    return jax.shard_map(
        functools.partial(body, nbits),
        mesh=mesh,
        in_specs=placed,
        out_specs=(P("dom", None), P("dom", None), P()),
        check_vma=False,
    )
```

```python
import functools

import jax
import jax.numpy as jnp
from jax import lax
from jax.experimental import pallas as pl
from jax.experimental.pallas import tpu as pltpu
from jax.sharding import PartitionSpec as P

MESH = pl.DeviceIdType.MESH
F32 = jnp.float32
BF16 = jnp.bfloat16


def bit_of(i, b):
    return lax.rem(lax.div(i, 1 << b), 2)


def flip(i, mask):
    out = i
    for b in range(mask.bit_length()):
        if mask >> b & 1:
            out = out + (1 - 2 * bit_of(i, b)) * (1 << b)
    return out


class Sems:
    def __init__(self, send, recv):
        self.send, self.recv, self.next = send, recv, 0

    def take(self):
        self.next += 1
        return self.next - 1


def names_and_shapes(tiles, block, width, entries, rounds, n_extra):
    nodes = tiles * block
    half, quarter, piece = width // 2, width // 8, width // 32
    v = pltpu.VMEM
    return dict(
        feat=v((tiles, block, width), BF16),
        wgt=v((width, width), BF16),
        gout=v((nodes, width), BF16),
        adj=v((entries, block, block), BF16),
        sfeat=v((rounds, block, width), BF16),
        sgrad=v((rounds, block, width), BF16),
        fsend=v((rounds, block, width), BF16),
        frecv=v((rounds, block, width), BF16),
        used=v((rounds, block, width), BF16),
        chain=v((entries + 1, block, block), F32),
        dense=v((nodes, (tiles + rounds) * block), BF16),
        part=v((nodes, width), F32),
        agg=v((nodes, width), BF16),
        outv=v((nodes, width), BF16),
        dpre=v((nodes, width), BF16),
        dagg=v((nodes, width), BF16),
        back=v((nodes, width), F32),
        gsend=v((rounds, block, width), BF16),
        grecv=v((rounds, block, width), BF16),
        gfeat=v((nodes, width), BF16),
        s0send=v((half, width), BF16),
        s0recv=v((half, width), BF16),
        acc=v((half, width), F32),
        s1send=v((half, width), BF16),
        s1recv=v((3, quarter, width), BF16),
        s2send=v((3, piece, width), BF16),
        s2recv=v((3, piece, width), BF16),
        xbuf=v((max(n_extra, 1), 4, piece, width), BF16),
        mine=v((piece, width), BF16),
        mixv=v((1, width), F32),
        row_s=pltpu.SMEM((1, entries), jnp.int32),
        src_s=pltpu.SMEM((1, entries), jnp.int32),
        tile_s=pltpu.SMEM((1, rounds), jnp.int32),
        lsem=pltpu.SemaphoreType.DMA((16,)),
        ssem=pltpu.SemaphoreType.DMA((96,)),
        rsem=pltpu.SemaphoreType.DMA((96,)),
    )


def kernel(names, nbits, *refs):
    (features, weight, grad_out, adjacency, stale_feat, stale_grad, blend,
     row_hbm, src_hbm, tile_hbm, tile_count, out_any, gf_any, gw_any) = refs[:14]
    s = dict(zip(names, refs[14:]))
    tile_row, tile_src, send_tile = s["row_s"], s["src_s"], s["tile_s"]
    tiles, block, width = s["feat"].shape
    rounds = s["fsend"].shape[0]
    entries = s["adj"].shape[0]
    nodes = tiles * block
    half, quarter, piece = width // 2, width // 8, width // 32
    me = lax.axis_index("dom")
    sems = Sems(s["ssem"], s["rsem"])
    pending = []

    def remote(src, dst, mask):
        i = sems.take()
        c = pltpu.make_async_remote_copy(
            src_ref=src, dst_ref=dst, send_sem=s["ssem"].at[i], recv_sem=s["rsem"].at[i],
            device_id=(flip(me, mask),), device_id_type=MESH)
        c.start()
        pending.append(c)
        return c

    loads = {}
    for i, (src, name) in enumerate((
            (tile_hbm, "tile_s"), (features, "feat"), (row_hbm, "row_s"), (src_hbm, "src_s"),
            (adjacency, "adj"), (blend, "mixv"), (stale_feat.at[0], "sfeat"),
            (weight, "wgt"), (grad_out, "gout"), (stale_grad.at[0], "sgrad"))):
        loads[name] = pltpu.make_async_copy(src, s[name], s["lsem"].at[i])
        loads[name].start()

    round_mask = [1 << (r * nbits // rounds) for r in range(rounds)]
    extra = []
    b = 5
    while b < nbits:
        extra.append((b, min(2, nbits - b)))
        b += 2
    peers = {1} | {k << 1 for k in (1, 2, 3)} | {k << 3 for k in (1, 2, 3)} | set(round_mask)
    for lo, nb in extra:
        peers |= {k << lo for k in range(1, 1 << nb)}
    barrier = pltpu.get_barrier_semaphore()
    for m in sorted(peers):
        pl.semaphore_signal(barrier, inc=1, device_id=(flip(me, m),), device_id_type=MESH)

    loads["tile_s"].wait()
    loads["feat"].wait()
    for r in range(rounds):
        s["fsend"][r] = s["feat"][send_tile[0, r]]
    pl.semaphore_wait(barrier, len(peers))
    fcopies = [remote(s["fsend"].at[r], s["frecv"].at[r], round_mask[r]) for r in range(rounds)]

    for name in ("row_s", "src_s"):
        loads[name].wait()
    live = tile_count[0]
    cells = tiles + rounds
    keys = [jnp.where(e < live, tile_row[0, e] * cells + tile_src[0, e], -1 - e) for e in range(entries)]
    loads["adj"].wait()
    s["chain"][0] = jnp.zeros((block, block), F32)
    for e in range(entries):
        prev = jnp.int32(0)
        for f in range(e):
            prev = jnp.where(keys[f] == keys[e], f + 1, prev)
        s["chain"][e + 1] = s["chain"][prev] + s["adj"][e].astype(F32)
    for t in range(tiles):
        for c in range(cells):
            last = jnp.int32(0)
            for e in range(entries):
                last = jnp.where(keys[e] == t * cells + c, e + 1, last)
            s["dense"][t * block:(t + 1) * block, c * block:(c + 1) * block] = s["chain"][last].astype(BF16)

    loads["mixv"].wait()
    mix = s["mixv"][...]
    keep = 1.0 - mix
    s["part"][...] = jnp.dot(s["dense"][:, :nodes], s["feat"][...].reshape(nodes, width),
                             preferred_element_type=F32)
    loads["sfeat"].wait()
    for r in range(rounds):
        fcopies[r].wait_recv()
        s["used"][r] = (keep * s["sfeat"][r].astype(F32) + mix * s["frecv"][r].astype(F32)).astype(BF16)
    loads["wgt"].wait()
    loads["gout"].wait()
    for t in range(tiles):
        rows = slice(t * block, (t + 1) * block)
        agg = (s["part"][rows, :] + jnp.dot(
            s["dense"][rows, nodes:], s["used"][...].reshape(rounds * block, width),
            preferred_element_type=F32)).astype(BF16)
        s["agg"][rows, :] = agg
        pre = jnp.dot(agg, s["wgt"][...], preferred_element_type=F32)
        sigma = jax.nn.sigmoid(pre)
        s["outv"][rows, :] = (pre * sigma).astype(BF16)
        s["dpre"][rows, :] = (s["gout"][rows, :].astype(F32) * sigma * (1.0 + pre * (1.0 - sigma))).astype(BF16)
    out_copy = pltpu.make_async_copy(s["outv"], out_any, s["lsem"].at[12])
    out_copy.start()

    j0 = bit_of(me, 0)
    j1 = lax.rem(lax.div(me, 2), 4)
    j2 = lax.rem(lax.div(me, 8), 4)

    def half_product(h):
        cols = pl.ds(pl.multiple_of(h * half, half), half)
        return lax.dot_general(s["agg"][:, cols], s["dpre"][...], (((0,), (0,)), ((), ())),
                               preferred_element_type=F32)

    def quarter_rows(k):
        return pl.ds(pl.multiple_of(flip(j1, k) * quarter, quarter), quarter)

    def piece_rows(k, base=0):
        return pl.ds(pl.multiple_of(base + flip(j2, k) * piece, piece), piece)

    s["s0send"][...] = half_product(1 - j0).astype(BF16)
    order1 = (3, 1, 2, 0)
    core = {}
    for k in order1:
        core[k] = remote(s["s0send"].at[quarter_rows(k)], s["s0recv"].at[quarter_rows(k)], 1)
    s["acc"][...] = half_product(j0)
    plane = {}
    for k in order1:
        core[k].wait_recv()
        total = s["acc"][quarter_rows(k), :] + s["s0recv"][quarter_rows(k), :].astype(F32)
        if k == 0:
            s["acc"][quarter_rows(0), :] = total
        else:
            s["s1send"][quarter_rows(k), :] = total.astype(BF16)
        if k == order1[2]:
            for kz in (3, 2, 1, 0):
                for kp in order1[:3]:
                    plane[kp, kz] = remote(s["s1send"].at[piece_rows(kz, flip(j1, kp) * quarter)],
                                           s["s1recv"].at[kp - 1, piece_rows(kz)], kp << 1)

    s["dagg"][...] = lax.dot_general(s["dpre"][...], s["wgt"][...], (((1,), (1,)), ((), ())),
                                     preferred_element_type=F32).astype(BF16)
    s["gsend"][...] = lax.dot_general(s["dense"][:, nodes:], s["dagg"][...], (((0,), (0,)), ((), ())),
                                      preferred_element_type=F32).astype(BF16).reshape(rounds, block, width)
    gcopies = {}
    late = [r for r in range(rounds) if round_mask[r] in (2, 4)]
    for r in range(rounds):
        if r not in late:
            gcopies[r] = remote(s["gsend"].at[r], s["grecv"].at[r], round_mask[r])
    s["back"][...] = lax.dot_general(s["dense"][:, :nodes], s["dagg"][...], (((0,), (0,)), ((), ())),
                                     preferred_element_type=F32)

    line = {}
    for kz in (3, 2, 1, 0):
        total = s["acc"][piece_rows(kz, j1 * quarter), :]
        for k in (1, 2, 3):
            plane[k, kz].wait_recv()
            total = total + s["s1recv"][k - 1, piece_rows(kz), :].astype(F32)
        if kz:
            s["s2send"][kz - 1] = total.astype(BF16)
            line[kz] = remote(s["s2send"].at[kz - 1], s["s2recv"].at[kz - 1], kz << 3)
    for r in late:
        gcopies[r] = remote(s["gsend"].at[r], s["grecv"].at[r], round_mask[r])
    loads["sgrad"].wait()
    hot = [[jnp.where(send_tile[0, r] == t, 1.0, 0.0).astype(F32) for r in range(rounds)] for t in range(tiles)]

    def mix_rounds(which, dst):
        for r in which:
            gcopies[r].wait_recv()
        for t in range(tiles):
            rows = slice(t * block, (t + 1) * block)
            acc = s["back"][rows, :]
            for r in which:
                acc = acc + hot[t][r] * (keep * s["sgrad"][r].astype(F32) + mix * s["grecv"][r].astype(F32))
            s[dst][rows, :] = acc.astype(s[dst].dtype)

    mix_rounds([r for r in range(rounds) if r not in late], "back")
    for kz in (1, 2, 3):
        line[kz].wait_recv()
        total = total + s["s2recv"][kz - 1].astype(F32)
    for g, (lo, nb) in enumerate(extra):
        size = 1 << nb
        jx = lax.rem(lax.div(me, 1 << lo), size)
        s["xbuf"][g, pl.ds(jx, 1)] = total.astype(BF16)[None]
        swaps = [remote(s["xbuf"].at[g, jx], s["xbuf"].at[g, jx], k << lo) for k in range(1, size)]
        for c in swaps:
            c.wait_recv()
        total = s["xbuf"][g, 0].astype(F32)
        for x in range(1, size):
            total = total + s["xbuf"][g, x].astype(F32)

    def gw_rows(kc, kp, kz):
        at = flip(j0, kc) * half + flip(j1, kp) * quarter + flip(j2, kz) * piece
        return pl.ds(pl.multiple_of(at, piece), piece)

    arrivals = {}

    def forward(kc, kp, kz, level):
        dst = gw_any.at[gw_rows(kc, kp, kz)]
        ref = s["mine"] if level > 2 else dst
        if level > 2:
            for k in (3, 2, 1):
                arrivals[kc, kp, k] = remote(ref, dst, k << 3)
        if level > 1:
            for k in (3, 1, 2):
                arrivals[kc, k, kz] = remote(ref, dst, k << 1)
        arrivals[1, kp, kz] = remote(ref, dst, 1)

    s["mine"][...] = total.astype(BF16)
    forward(0, 0, 0, 3)
    own = pltpu.make_async_copy(s["mine"], gw_any.at[gw_rows(0, 0, 0)], s["lsem"].at[14])
    own.start()

    mix_rounds(late, "gfeat")
    gf_copy = pltpu.make_async_copy(s["gfeat"], gf_any, s["lsem"].at[13])
    gf_copy.start()

    for kz in (1, 2, 3):
        arrivals[0, 0, kz].wait_recv()
        forward(0, 0, kz, 2)
    for kz in (0, 1, 2, 3):
        for kp in (1, 2, 3):
            arrivals[0, kp, kz].wait_recv()
            forward(0, kp, kz, 1)
    for kz in range(4):
        for kp in range(4):
            arrivals[1, kp, kz].wait_recv()
    for c in pending:
        c.wait_send()
    own.wait()
    out_copy.wait()
    gf_copy.wait()


def finish(*refs):
    ins, outs, sem = refs[:3], refs[3:6], refs[6]
    parts = 4
    copies = []
    for i, (a, b) in enumerate(zip(ins, outs)):
        step = a.shape[0] // parts
        for q in range(parts):
            rows = pl.ds(q * step, step)
            copies.append(pltpu.make_async_copy(a.at[rows], b.at[rows], sem.at[i * parts + q]))
    for c in copies:
        c.start()
    for c in copies:
        c.wait()


def body(nbits, features, weight, grad_out, adjacency, tile_row, tile_src, tile_count,
         send_tile, stale_feat, stale_grad, blend):
    nodes, width = features.shape
    entries, block = adjacency.shape[:2]
    rounds = send_tile.shape[1]
    tiles = nodes // block
    n_extra = (max(nbits - 5, 0) + 1) // 2
    scratch = names_and_shapes(tiles, block, width, entries, rounds, n_extra)
    hbm = pl.BlockSpec(memory_space=pltpu.HBM)
    free = pl.BlockSpec(memory_space=pl.ANY)
    results = (jax.ShapeDtypeStruct((nodes, width), BF16),
               jax.ShapeDtypeStruct((nodes, width), BF16),
               jax.ShapeDtypeStruct((width, width), BF16))
    found = pl.pallas_call(
        functools.partial(kernel, tuple(scratch), nbits),
        name="layer",
        out_shape=results,
        in_specs=[hbm] * 10 + [pl.BlockSpec(memory_space=pltpu.SMEM)],
        out_specs=(free,) * 3,
        scratch_shapes=list(scratch.values()),
        compiler_params=pltpu.CompilerParams(collective_id=0, has_side_effects=True,
                                             vmem_limit_bytes=48 * 1024 * 1024),
    )(*(pltpu.with_memory_space_constraint(x, pltpu.HBM) for x in (
        features.reshape(tiles, block, width), weight, grad_out, adjacency, stale_feat, stale_grad,
        blend.reshape(1, width), tile_row, tile_src, send_tile)), tile_count)
    return tuple(pl.pallas_call(
        finish,
        name="finish",
        out_shape=results,
        in_specs=[free] * 3,
        out_specs=(hbm,) * 3,
        scratch_shapes=[pltpu.SemaphoreType.DMA((12,))],
        compiler_params=pltpu.CompilerParams(vmem_limit_bytes=16 * 1024 * 1024),
    )(*found))


def solution(mesh):
    nbits = mesh.shape["dom"].bit_length() - 1
    placed = (
        P("dom", None), P(), P("dom", None), P("dom", None, None), P("dom", None), P("dom", None),
        P("dom"), P("dom", None), P("dom", None, None, None), P("dom", None, None, None), P(),
    )
    return jax.shard_map(
        functools.partial(body, nbits),
        mesh=mesh,
        in_specs=placed,
        out_specs=(P("dom", None), P("dom", None), P()),
        check_vma=False,
    )
```

```python
import functools

import jax
import jax.numpy as jnp
from jax import lax
from jax.experimental import pallas as pl
from jax.experimental.pallas import tpu as pltpu
from jax.sharding import PartitionSpec as P

MESH = pl.DeviceIdType.MESH
F32 = jnp.float32
BF16 = jnp.bfloat16


def bit_of(i, b):
    return lax.rem(lax.div(i, 1 << b), 2)


def flip(i, mask):
    out = i
    for b in range(mask.bit_length()):
        if mask >> b & 1:
            out = out + (1 - 2 * bit_of(i, b)) * (1 << b)
    return out


class Sems:
    def __init__(self, send, recv):
        self.send, self.recv, self.next = send, recv, 0

    def take(self):
        self.next += 1
        return self.next - 1


def names_and_shapes(tiles, block, width, entries, rounds, n_extra):
    nodes = tiles * block
    half, quarter, piece = width // 2, width // 8, width // 32
    v = pltpu.VMEM
    return dict(
        feat=v((tiles, block, width), BF16),
        wgt=v((width, width), BF16),
        gout=v((nodes, width), BF16),
        adj=v((entries, block, block), BF16),
        sfeat=v((rounds, block, width), BF16),
        sgrad=v((rounds, block, width), BF16),
        fsend=v((rounds, block, width), BF16),
        frecv=v((rounds, block, width), BF16),
        used=v((rounds, block, width), BF16),
        chain=v((entries + 1, block, block), F32),
        dense=v((nodes, (tiles + rounds) * block), BF16),
        part=v((nodes, width), F32),
        agg=v((nodes, width), BF16),
        outv=v((nodes, width), BF16),
        dpre=v((nodes, width), BF16),
        dagg=v((nodes, width), BF16),
        back=v((nodes, width), F32),
        gsend=v((rounds, block, width), BF16),
        grecv=v((rounds, block, width), BF16),
        gfeat=v((nodes, width), BF16),
        s0send=v((half, width), BF16),
        s0recv=v((half, width), BF16),
        acc=v((half, width), F32),
        s1send=v((half, width), BF16),
        s1recv=v((3, quarter, width), BF16),
        s2send=v((3, piece, width), BF16),
        s2recv=v((3, piece, width), BF16),
        xbuf=v((max(n_extra, 1), 4, piece, width), BF16),
        mine=v((piece, width), BF16),
        mixv=v((1, width), F32),
        row_s=pltpu.SMEM((1, entries), jnp.int32),
        src_s=pltpu.SMEM((1, entries), jnp.int32),
        tile_s=pltpu.SMEM((1, rounds), jnp.int32),
        lsem=pltpu.SemaphoreType.DMA((16,)),
        ssem=pltpu.SemaphoreType.DMA((96,)),
        rsem=pltpu.SemaphoreType.DMA((96,)),
    )


def kernel(names, nbits, *refs):
    (features, weight, grad_out, adjacency, stale_feat, stale_grad, blend,
     row_hbm, src_hbm, tile_hbm, tile_count, out_any, gf_any, gw_any) = refs[:14]
    s = dict(zip(names, refs[14:]))
    tile_row, tile_src, send_tile = s["row_s"], s["src_s"], s["tile_s"]
    tiles, block, width = s["feat"].shape
    rounds = s["fsend"].shape[0]
    entries = s["adj"].shape[0]
    nodes = tiles * block
    half, quarter, piece = width // 2, width // 8, width // 32
    me = lax.axis_index("dom")
    sems = Sems(s["ssem"], s["rsem"])
    pending = []

    def remote(src, dst, mask):
        i = sems.take()
        c = pltpu.make_async_remote_copy(
            src_ref=src, dst_ref=dst, send_sem=s["ssem"].at[i], recv_sem=s["rsem"].at[i],
            device_id=(flip(me, mask),), device_id_type=MESH)
        c.start()
        pending.append(c)
        return c

    loads = {}
    for i, (src, name) in enumerate((
            (tile_hbm, "tile_s"), (features, "feat"), (row_hbm, "row_s"), (src_hbm, "src_s"),
            (adjacency, "adj"), (blend, "mixv"), (stale_feat.at[0], "sfeat"),
            (weight, "wgt"), (grad_out, "gout"), (stale_grad.at[0], "sgrad"))):
        loads[name] = pltpu.make_async_copy(src, s[name], s["lsem"].at[i])
        loads[name].start()

    round_mask = [1 << (r * nbits // rounds) for r in range(rounds)]
    extra = []
    b = 5
    while b < nbits:
        extra.append((b, min(2, nbits - b)))
        b += 2
    peers = {1} | {k << 1 for k in (1, 2, 3)} | {k << 3 for k in (1, 2, 3)} | set(round_mask)
    for lo, nb in extra:
        peers |= {k << lo for k in range(1, 1 << nb)}
    barrier = pltpu.get_barrier_semaphore()
    for m in sorted(peers):
        pl.semaphore_signal(barrier, inc=1, device_id=(flip(me, m),), device_id_type=MESH)

    loads["tile_s"].wait()
    loads["feat"].wait()
    for r in range(rounds):
        s["fsend"][r] = s["feat"][send_tile[0, r]]
    pl.semaphore_wait(barrier, len(peers))
    fcopies = [remote(s["fsend"].at[r], s["frecv"].at[r], round_mask[r]) for r in range(rounds)]

    for name in ("row_s", "src_s"):
        loads[name].wait()
    live = tile_count[0]
    cells = tiles + rounds
    keys = [jnp.where(e < live, tile_row[0, e] * cells + tile_src[0, e], -1 - e) for e in range(entries)]
    loads["adj"].wait()
    s["chain"][0] = jnp.zeros((block, block), F32)
    for e in range(entries):
        prev = jnp.int32(0)
        for f in range(e):
            prev = jnp.where(keys[f] == keys[e], f + 1, prev)
        s["chain"][e + 1] = s["chain"][prev] + s["adj"][e].astype(F32)
    for t in range(tiles):
        for c in range(cells):
            last = jnp.int32(0)
            for e in range(entries):
                last = jnp.where(keys[e] == t * cells + c, e + 1, last)
            s["dense"][t * block:(t + 1) * block, c * block:(c + 1) * block] = s["chain"][last].astype(BF16)

    loads["mixv"].wait()
    mix = s["mixv"][...]
    keep = 1.0 - mix
    s["part"][...] = jnp.dot(s["dense"][:, :nodes], s["feat"][...].reshape(nodes, width),
                             preferred_element_type=F32)
    loads["sfeat"].wait()
    for r in range(rounds):
        fcopies[r].wait_recv()
        s["used"][r] = (keep * s["sfeat"][r].astype(F32) + mix * s["frecv"][r].astype(F32)).astype(BF16)
    loads["wgt"].wait()
    loads["gout"].wait()
    for t in range(tiles):
        rows = slice(t * block, (t + 1) * block)
        agg = (s["part"][rows, :] + jnp.dot(
            s["dense"][rows, nodes:], s["used"][...].reshape(rounds * block, width),
            preferred_element_type=F32)).astype(BF16)
        s["agg"][rows, :] = agg
        pre = jnp.dot(agg, s["wgt"][...], preferred_element_type=F32)
        sigma = jax.nn.sigmoid(pre)
        s["outv"][rows, :] = (pre * sigma).astype(BF16)
        s["dpre"][rows, :] = (s["gout"][rows, :].astype(F32) * sigma * (1.0 + pre * (1.0 - sigma))).astype(BF16)
    out_copy = pltpu.make_async_copy(s["outv"], out_any, s["lsem"].at[12])
    out_copy.start()

    j0 = bit_of(me, 0)
    j1 = lax.rem(lax.div(me, 2), 4)
    j2 = lax.rem(lax.div(me, 8), 4)

    def half_product(h):
        cols = pl.ds(pl.multiple_of(h * half, half), half)
        return lax.dot_general(s["agg"][:, cols], s["dpre"][...], (((0,), (0,)), ((), ())),
                               preferred_element_type=F32)

    def quarter_rows(k):
        return pl.ds(pl.multiple_of(flip(j1, k) * quarter, quarter), quarter)

    def piece_rows(k, base=0):
        return pl.ds(pl.multiple_of(base + flip(j2, k) * piece, piece), piece)

    s["s0send"][...] = half_product(1 - j0).astype(BF16)
    order1 = (3, 1, 2, 0)
    core = {}
    for k in order1:
        core[k] = remote(s["s0send"].at[quarter_rows(k)], s["s0recv"].at[quarter_rows(k)], 1)
    s["acc"][...] = half_product(j0)
    plane = {}
    for k in order1:
        core[k].wait_recv()
        total = s["acc"][quarter_rows(k), :] + s["s0recv"][quarter_rows(k), :].astype(F32)
        if k == 0:
            s["acc"][quarter_rows(0), :] = total
        else:
            s["s1send"][quarter_rows(k), :] = total.astype(BF16)
        if k == order1[2]:
            for kz in (3, 2, 1, 0):
                for kp in order1[:3]:
                    plane[kp, kz] = remote(s["s1send"].at[piece_rows(kz, flip(j1, kp) * quarter)],
                                           s["s1recv"].at[kp - 1, piece_rows(kz)], kp << 1)

    s["dagg"][...] = lax.dot_general(s["dpre"][...], s["wgt"][...], (((1,), (1,)), ((), ())),
                                     preferred_element_type=F32).astype(BF16)
    s["gsend"][...] = lax.dot_general(s["dense"][:, nodes:], s["dagg"][...], (((0,), (0,)), ((), ())),
                                      preferred_element_type=F32).astype(BF16).reshape(rounds, block, width)
    gcopies = {}
    late = [r for r in range(rounds) if round_mask[r] in (2, 4)]
    for r in [r for r in range(rounds) if r not in late] + late:
        gcopies[r] = remote(s["gsend"].at[r], s["grecv"].at[r], round_mask[r])
    s["back"][...] = lax.dot_general(s["dense"][:, :nodes], s["dagg"][...], (((0,), (0,)), ((), ())),
                                     preferred_element_type=F32)

    line = {}
    for kz in (3, 2, 1, 0):
        total = s["acc"][piece_rows(kz, j1 * quarter), :]
        for k in (1, 2, 3):
            plane[k, kz].wait_recv()
            total = total + s["s1recv"][k - 1, piece_rows(kz), :].astype(F32)
        if kz:
            s["s2send"][kz - 1] = total.astype(BF16)
            line[kz] = remote(s["s2send"].at[kz - 1], s["s2recv"].at[kz - 1], kz << 3)
    loads["sgrad"].wait()
    hot = [[jnp.where(send_tile[0, r] == t, 1.0, 0.0).astype(F32) for r in range(rounds)] for t in range(tiles)]

    def mix_rounds(which, dst):
        for r in which:
            gcopies[r].wait_recv()
        for t in range(tiles):
            rows = slice(t * block, (t + 1) * block)
            acc = s["back"][rows, :]
            for r in which:
                acc = acc + hot[t][r] * (keep * s["sgrad"][r].astype(F32) + mix * s["grecv"][r].astype(F32))
            s[dst][rows, :] = acc.astype(s[dst].dtype)

    mix_rounds([r for r in range(rounds) if r not in late], "back")
    for kz in (1, 2, 3):
        line[kz].wait_recv()
        total = total + s["s2recv"][kz - 1].astype(F32)
    for g, (lo, nb) in enumerate(extra):
        size = 1 << nb
        jx = lax.rem(lax.div(me, 1 << lo), size)
        s["xbuf"][g, pl.ds(jx, 1)] = total.astype(BF16)[None]
        swaps = [remote(s["xbuf"].at[g, jx], s["xbuf"].at[g, jx], k << lo) for k in range(1, size)]
        for c in swaps:
            c.wait_recv()
        total = s["xbuf"][g, 0].astype(F32)
        for x in range(1, size):
            total = total + s["xbuf"][g, x].astype(F32)

    def gw_rows(kc, kp, kz):
        at = flip(j0, kc) * half + flip(j1, kp) * quarter + flip(j2, kz) * piece
        return pl.ds(pl.multiple_of(at, piece), piece)

    arrivals = {}

    def forward(kc, kp, kz, level):
        dst = gw_any.at[gw_rows(kc, kp, kz)]
        ref = s["mine"] if level > 2 else dst
        if level > 2:
            for k in (3, 2, 1):
                arrivals[kc, kp, k] = remote(ref, dst, k << 3)
        if level > 1:
            for k in (3, 1, 2):
                arrivals[kc, k, kz] = remote(ref, dst, k << 1)
        arrivals[1, kp, kz] = remote(ref, dst, 1)

    s["mine"][...] = total.astype(BF16)
    forward(0, 0, 0, 3)
    own = pltpu.make_async_copy(s["mine"], gw_any.at[gw_rows(0, 0, 0)], s["lsem"].at[14])
    own.start()

    mix_rounds(late, "gfeat")
    gf_copy = pltpu.make_async_copy(s["gfeat"], gf_any, s["lsem"].at[13])
    gf_copy.start()

    for kz in (1, 2, 3):
        arrivals[0, 0, kz].wait_recv()
        forward(0, 0, kz, 2)
    for kz in (0, 1, 2, 3):
        for kp in (1, 2, 3):
            arrivals[0, kp, kz].wait_recv()
            forward(0, kp, kz, 1)
    for kz in range(4):
        for kp in range(4):
            arrivals[1, kp, kz].wait_recv()
    for c in pending:
        c.wait_send()
    own.wait()
    out_copy.wait()
    gf_copy.wait()


def finish(*refs):
    ins, outs, sem = refs[:3], refs[3:6], refs[6]
    parts = 1
    copies = []
    for i, (a, b) in enumerate(zip(ins, outs)):
        step = a.shape[0] // parts
        for q in range(parts):
            rows = pl.ds(q * step, step)
            copies.append(pltpu.make_async_copy(a.at[rows], b.at[rows], sem.at[i * parts + q]))
    for c in copies:
        c.start()
    for c in copies:
        c.wait()


def body(nbits, features, weight, grad_out, adjacency, tile_row, tile_src, tile_count,
         send_tile, stale_feat, stale_grad, blend):
    nodes, width = features.shape
    entries, block = adjacency.shape[:2]
    rounds = send_tile.shape[1]
    tiles = nodes // block
    n_extra = (max(nbits - 5, 0) + 1) // 2
    scratch = names_and_shapes(tiles, block, width, entries, rounds, n_extra)
    hbm = pl.BlockSpec(memory_space=pltpu.HBM)
    free = pl.BlockSpec(memory_space=pl.ANY)
    results = (jax.ShapeDtypeStruct((nodes, width), BF16),
               jax.ShapeDtypeStruct((nodes, width), BF16),
               jax.ShapeDtypeStruct((width, width), BF16))
    found = pl.pallas_call(
        functools.partial(kernel, tuple(scratch), nbits),
        name="layer",
        out_shape=results,
        in_specs=[hbm] * 10 + [pl.BlockSpec(memory_space=pltpu.SMEM)],
        out_specs=(free,) * 3,
        scratch_shapes=list(scratch.values()),
        compiler_params=pltpu.CompilerParams(collective_id=0, has_side_effects=True,
                                             vmem_limit_bytes=48 * 1024 * 1024),
    )(*(pltpu.with_memory_space_constraint(x, pltpu.HBM) for x in (
        features.reshape(tiles, block, width), weight, grad_out, adjacency, stale_feat, stale_grad,
        blend.reshape(1, width), tile_row, tile_src, send_tile)), tile_count)
    return tuple(pl.pallas_call(
        finish,
        name="finish",
        out_shape=results,
        in_specs=[free] * 3,
        out_specs=(hbm,) * 3,
        scratch_shapes=[pltpu.SemaphoreType.DMA((3,))],
        compiler_params=pltpu.CompilerParams(vmem_limit_bytes=16 * 1024 * 1024),
    )(*found))


def solution(mesh):
    nbits = mesh.shape["dom"].bit_length() - 1
    placed = (
        P("dom", None), P(), P("dom", None), P("dom", None, None), P("dom", None), P("dom", None),
        P("dom"), P("dom", None), P("dom", None, None, None), P("dom", None, None, None), P(),
    )
    return jax.shard_map(
        functools.partial(body, nbits),
        mesh=mesh,
        in_specs=placed,
        out_specs=(P("dom", None), P("dom", None), P()),
        check_vma=False,
    )
```
